32 devices in a mesh: groups: 2 (over y), ctx: 16 (over z, x, core).
Axes of the slice: x: 2, y: 2, z: 4, core: 2. Of those that a mesh axis runs over, the one named last changes fastest.
Arguments:
- queries: bfloat16 [64, 8192], P('groups'), parts along dimension 0, may hold values from -12 to 12
- keys: bfloat16 [32768, 1024], P(('groups', 'ctx')), parts along dimension 0, may hold values from -6 to 6
- values: bfloat16 [32768, 1024], P(('groups', 'ctx')), parts along dimension 0, may hold values from -6 to 6
- valid_len: int32 [32], P('groups'), parts along dimension 0, may hold values from 1 to 1024, 12288 in all
- row_counts: int32 [8], P('groups'), parts along dimension 0, may hold values from 1 to 8, 24 in all
- out_weight: bfloat16 [8192, 8192], P('ctx'), may hold values from -0.25 to 0.25
Outputs:
- attended: bfloat16 [64, 8192], P('groups', 'ctx'), parts along dimension 0
The draws below stay inside these ranges and needn't reach their ends.
There are 2 independent parts, one for each index of `groups`. The reference program is written for one: setup_inputs(seed, part) draws one part's arguments, and reference() takes and returns one part's arrays. A program takes and returns all parts, laid end to end along the dimension named above; an argument that names none is the same for every part. Nothing has to cross between parts.
Inputs may be any that keep to these rules, and one draw needn't show every extreme that they name: `valid_len`: positions in use are the first ones of each shard; every shard uses at least one, and one shard uses all 1024. `row_counts`: the first rows of each batch are live, the others are padding; the counts sum to 24 and one batch is full.
All inputs are finite; a program needn't handle non-finite values.
Results may differ from the reference program's by a relative error of at most 0.0049.
Values may be sent and summed in bfloat16 or wider, within the bound.
A program may use at most 64 MiB of HBM per device.

```python
import math
import jax
import jax.numpy as jnp
import numpy as np
from jax import lax

HEADS = 64
KVH = 8
HD = 128
D = 8192
CTX_DEV = 1024
BATCH_ROWS = 8
NBATCH = 4
ROWS = 32
SHARDS = 16
PREFIX = 16384


def draw_queries(key, part):
    drawn = jax.random.truncated_normal(jax.random.fold_in(key, 11), -4.0, 4.0, (ROWS, HEADS * HD), jnp.float32) * 3.0
    return drawn.astype(jnp.bfloat16)


def draw_keys(key, part):
    drawn = jax.random.truncated_normal(jax.random.fold_in(key, 21), -6.0, 6.0, (PREFIX, KVH * HD), jnp.float32)
    return drawn.astype(jnp.bfloat16)


def raised(entries, key, source, target, parts, factor):
    def block_of(position):
        return (jnp.arange(entries.shape[position]) // (entries.shape[position] // parts)).reshape((-1,) + (1,) * (entries.ndim - 1 - position))

    one_side = jax.random.permutation(key, parts)[block_of(target)]
    far = (block_of(target) + parts // 2) % parts
    return jnp.where((block_of(source) == one_side) | (block_of(source) == far), factor * entries, entries)


def block_scale(rng, dims, cuts, low, top_value):
    loudness, own = 1.0, jax.random.fold_in(rng, 6)
    for axis_at, parts in cuts:
        draws = jnp.exp(jax.random.uniform(jax.random.fold_in(own, axis_at), (parts,), jnp.float32, low / len(cuts), top_value / len(cuts)))
        loudness = loudness * jnp.repeat(draws, dims[axis_at] // parts).reshape([-1 if axis == axis_at else 1 for axis in range(len(dims))])
    return loudness


def split_up(count, total, bound, slope):
    portions = [(1 << 20) // math.isqrt(grade ** slope) + 1 for grade in range(2, count + 1)]
    spare, holding = total - bound - (count - 1), [1] * (count - 1)
    while spare > 0:
        free = [i for i in range(count - 1) if holding[i] < bound]
        whole, left = sum([portions[i] for i in free]), spare
        for i in free:
            extra = min(bound - holding[i], max(1, left * portions[i] // whole), spare)
            holding[i] = holding[i] + extra
            spare = spare - extra
    return np.array([bound] + holding)


def uneven_parts(stream_key, count, total, reach, slope):
    if count == 2:
        one = jax.random.randint(stream_key, (), max(1, total - reach), min(reach, total - 1) + 1)
        return jnp.stack([one, total - one])
    sizes = jnp.asarray(split_up(count, total, reach, slope), jnp.int32)
    couples = (count - 1) // 2
    source_of, sink = sizes[1:1 + 2 * couples:2], sizes[2:2 + 2 * couples:2]
    room = jnp.minimum(source_of - 1, reach - sink)
    shifted = jax.random.randint(jax.random.fold_in(stream_key, 1), (couples,), 0, 1 << 20) % (room + 1)
    sizes = sizes.at[1:1 + 2 * couples:2].set(source_of - shifted).at[2:2 + 2 * couples:2].set(sink + shifted)
    return sizes[jax.random.permutation(jax.random.fold_in(stream_key, 2), count)]


def scatter_about(own_key, extent, deviation, limit, pieces=(), kind=jnp.bfloat16):
    loudness = block_scale(own_key, extent, pieces, -0.22, 0.18) if pieces else 1.0
    values = jax.random.normal(own_key, extent, jnp.float32) * deviation * loudness
    return jnp.minimum(jnp.maximum(values, -limit), limit).astype(kind)


def noise_with(rng, shape, scale, reach, split, heavy, kind=jnp.bfloat16):
    values = scale * jax.random.normal(rng, shape, jnp.float32)
    if split:
        values = values * block_scale(rng, shape, split, -0.22, 0.18)
    return jnp.clip(raised(values, jax.random.fold_in(rng, 3), *heavy), -reach, reach).astype(kind)


def setup_inputs(seed: int = 0, part: int = 0) -> dict:
    streams_of = jax.random.split(jax.random.key(seed), 7)
    part_splits = jax.random.split(jax.random.fold_in(streams_of[6], part), 7)
    return {
        "queries": draw_queries(jax.random.fold_in(jax.random.fold_in(streams_of[6], part), 71), part),
        "keys": draw_keys(jax.random.fold_in(jax.random.fold_in(streams_of[6], part), 71), part),
        "values": scatter_about(part_splits[2], (PREFIX, KVH * HD), 1.0, 6.0, ((0, 16),)),
        "valid_len": uneven_parts(part_splits[3], SHARDS, SHARDS * CTX_DEV * 3 // 4, CTX_DEV, 0).astype(jnp.int32),
        "row_counts": uneven_parts(part_splits[4], NBATCH, 3 * BATCH_ROWS, BATCH_ROWS, 0).astype(jnp.int32),
        "out_weight": noise_with(streams_of[5], (HEADS * HD, D), (HEADS * HD // 8) ** -0.5, 0.25, ((0, 16),), (0, 1, 16, 2.0)),
    }


def reference(queries, keys, values, valid_len, row_counts, out_weight):
    per_kv = HEADS // KVH
    inv_root = 1.0 / math.sqrt(HD)
    query_heads = queries.reshape(ROWS, KVH, per_kv, HD).astype(jnp.float32)
    key_blocks = keys.reshape(SHARDS, CTX_DEV, KVH, HD)
    value_blocks = values.reshape(SHARDS, CTX_DEV, KVH, HD)
    positions = jnp.arange(CTX_DEV, dtype=jnp.int32)

    def absorb(running, shard_data):
        run_max, weighted, merge_sum = running
        key_block, value_block, valid_count = shard_data
        scores = jnp.einsum('rkgd,pkd->rkgp', query_heads, key_block.astype(jnp.float32)) * inv_root
        scores = jnp.where(positions < valid_count, scores, -jnp.inf)
        peak = lax.optimization_barrier(jnp.max(scores, axis=-1, keepdims=True))
        exp_scores = jnp.exp(scores - peak)
        expo_sum = lax.optimization_barrier(jnp.sum(exp_scores, axis=-1))
        weights = lax.optimization_barrier(exp_scores.astype(jnp.bfloat16)).astype(jnp.float32)
        head_out = jnp.einsum('rkgp,pkd->rkgd', weights, value_block.astype(jnp.float32)) / expo_sum[..., None]
        log_sum = peak[..., 0] + jnp.log(expo_sum)
        new_max = jnp.maximum(run_max, log_sum)
        old_scale = jnp.exp(run_max - new_max)
        new_scale = jnp.exp(log_sum - new_max)
        weighted = weighted * old_scale[..., None] + new_scale[..., None] * head_out
        merge_sum = merge_sum * old_scale + new_scale
        return ((new_max, weighted, merge_sum), None)
    start = (jnp.full((ROWS, KVH, per_kv), -jnp.inf, jnp.float32), jnp.zeros((ROWS, KVH, per_kv, HD), jnp.float32), jnp.zeros((ROWS, KVH, per_kv), jnp.float32))
    final, unused = lax.scan(absorb, start, (key_blocks, value_blocks, valid_len.astype(jnp.int32)))
    merged = (final[1] / final[2][..., None]).reshape(ROWS, HEADS * HD).astype(jnp.bfloat16)
    projected = jnp.dot(merged, out_weight, preferred_element_type=jnp.float32)
    row_ids = jnp.arange(ROWS, dtype=jnp.int32)
    live_rows = row_ids % BATCH_ROWS < row_counts[row_ids // BATCH_ROWS]
    return jnp.where(live_rows[:, None], projected, 0.0).astype(jnp.bfloat16)
```

```python
import functools
import math

import jax
import jax.numpy as jnp
from jax import lax
from jax.experimental import pallas as pl
from jax.experimental.pallas import tpu as pltpu
from jax.sharding import PartitionSpec as P

HEADS = 64
KVH = 8
HD = 128
BATCH_ROWS = 8
NBATCH = 4
LIVE_ROWS = 24


def on_device(queries, keys, values, valid_len, row_counts, out_weight):
    shards = lax.axis_size("ctx")
    my_index = lax.axis_index("ctx")
    ctx_rows = keys.shape[0]
    per_kv = HEADS // KVH
    head_width = per_kv * HD
    col_width = HEADS * HD // shards
    slot_width = max(HEADS, shards) // shards
    inv_root = 1.0 / math.sqrt(HD)
    own_count = jnp.sum(jnp.where(jnp.arange(shards, dtype=jnp.int32) == my_index, valid_len, 0))
    key_valid = jnp.arange(ctx_rows, dtype=jnp.int32) < own_count
    num_rows = queries.shape[0]
    outputs = []
    log_sums = []
    for kv_index in range(KVH):
        query_block = queries[:, kv_index * head_width : (kv_index + 1) * head_width].reshape(
            num_rows, per_kv, HD
        )
        key_block = keys[:, kv_index * HD : (kv_index + 1) * HD]
        value_block = values[:, kv_index * HD : (kv_index + 1) * HD]
        scores = (
            jnp.einsum("rgd,pd->rgp", query_block, key_block, preferred_element_type=jnp.float32)
            * inv_root
        )
        scores = jnp.where(key_valid, scores, -jnp.inf)
        peak = jnp.max(scores, axis=-1, keepdims=True)
        exp_scores = jnp.exp(scores - peak)
        expo_sum = jnp.sum(exp_scores, axis=-1)
        weights = exp_scores.astype(jnp.bfloat16)
        head_out = (
            jnp.einsum("rgp,pd->rgd", weights, value_block, preferred_element_type=jnp.float32)
            / expo_sum[..., None]
        )
        outputs.append(head_out.reshape(num_rows, head_width))
        log_sums.append(peak[..., 0] + jnp.log(expo_sum))
    partial_value, log_sums = (jnp.concatenate(outputs, axis=1), jnp.concatenate(log_sums, axis=1))
    slot_sums = jnp.repeat(log_sums, max(1, shards // HEADS), axis=1)
    combine_partial_value = lax.all_to_all(
        partial_value[None], "ctx", split_axis=2, concat_axis=0, tiled=True
    )
    combine_slot_sums = lax.all_to_all(
        slot_sums[None], "ctx", split_axis=2, concat_axis=0, tiled=True
    )
    biggest = jnp.max(combine_slot_sums, axis=0, keepdims=True)
    merge_wts = jnp.exp(combine_slot_sums - biggest)
    merge_sum = jnp.sum(merge_wts, axis=0)
    spread_wts = jnp.repeat(merge_wts, col_width // slot_width, axis=2)
    merged = jnp.sum(spread_wts * combine_partial_value, axis=0) / jnp.repeat(
        merge_sum, col_width // slot_width, axis=1
    )
    project_merged = merged.astype(jnp.bfloat16)
    term = jnp.dot(project_merged, out_weight, preferred_element_type=jnp.float32)
    projected = lax.psum_scatter(term, "ctx", scatter_dimension=1, tiled=True)
    row_ids = jnp.arange(queries.shape[0], dtype=jnp.int32)
    batch_ids = row_ids // BATCH_ROWS
    row_limit = jnp.sum(
        jnp.where(
            batch_ids[:, None] == jnp.arange(NBATCH, dtype=jnp.int32)[None, :],
            row_counts[None, :],
            0,
        ),
        axis=1,
    )
    live_rows = row_ids % BATCH_ROWS < row_limit
    return jnp.where(live_rows[:, None], projected, 0.0).astype(jnp.bfloat16)


def fused_kernel(
    shards,
    lens_hbm,
    counts_hbm,
    q_hbm,
    k_hbm,
    v_hbm,
    w_hbm,
    out_ref,
    lens_ref,
    counts_ref,
    q_s,
    k_s,
    v_s,
    w_s,
    num_own,
    stat_own,
    core_send,
    core_recv,
    core_stat_send,
    core_stat_recv,
    mid_send,
    mid_recv,
    mid_stat_send,
    mid_stat_recv,
    top_send,
    top_recv,
    top_stat_send,
    top_stat_recv,
    term_own,
    tcore_send,
    tcore_recv,
    tmid_send,
    tmid_recv,
    ttop_send,
    ttop_recv,
    int_sem,
    q_sem,
    k_sem,
    v_sem,
    w_sem,
    core_ss,
    core_rs,
    mid_ss,
    mid_rs,
    top_ss,
    top_rs,
    tcore_ss,
    tcore_rs,
    tmid_ss,
    tmid_rs,
    ttop_ss,
    ttop_rs,
):
    me = lax.axis_index("ctx")
    tops = shards // 4
    core, mid, top = me % 2, (me // 2) % 2, me // 4
    chips = 2 * tops
    num_rows = q_hbm.shape[0]
    half_heads = HEADS // KVH // 2
    half = half_heads * HD
    width = w_hbm.shape[1] // shards
    ctx_rows = k_hbm.shape[0]

    apart = list(range(tops - 1, 0, -1))
    order = [(1, d) for d in apart] + [(0, d) for d in apart] + [(1, 0), (0, 0)]

    def top_at(d):
        place = 0
        bit = 1
        while bit < tops:
            place = place + bit * ((top // bit + d // bit) % 2)
            bit *= 2
        return place

    def chip_of(i):
        flip, d = order[i]
        return top_at(d) * 2 + (mid + flip) % 2

    core_peer = me + 1 - 2 * core
    mid_peer = me + 2 - 4 * mid

    def top_peer(d):
        return top_at(d) * 4 + mid * 2 + core

    loads = []
    for i in range(chips):
        kv = chip_of(i)
        first = pl.multiple_of(kv * 2 * half + core * half, half)
        second = pl.multiple_of(kv * 2 * half + (1 - core) * half, half)
        cols = pl.ds(pl.multiple_of(kv * HD, HD), HD)
        loads.append(
            (
                pltpu.make_async_copy(q_hbm.at[:, pl.ds(first, half)], q_s.at[i, 0], q_sem.at[i, 0]),
                pltpu.make_async_copy(q_hbm.at[:, pl.ds(second, half)], q_s.at[i, 1], q_sem.at[i, 1]),
                pltpu.make_async_copy(k_hbm.at[:, cols], k_s.at[i], k_sem.at[i]),
                pltpu.make_async_copy(v_hbm.at[:, cols], v_s.at[i], v_sem.at[i]),
            )
        )
    ints = (
        pltpu.make_async_copy(lens_hbm, lens_ref, int_sem.at[0]),
        pltpu.make_async_copy(counts_hbm, counts_ref, int_sem.at[1]),
    )
    for copy in loads[0] + ints + loads[1]:
        copy.start()
    w_loads = []
    for i in range(chips):
        pair = []
        for side in range(2):
            owner = chip_of(i) * 2 + (1 - core if side == 0 else core)
            cols = pl.ds(pl.multiple_of(owner * width, width), width)
            pair.append(pltpu.make_async_copy(w_hbm.at[:, cols], w_s.at[i, side], w_sem.at[i, side]))
        w_loads.append(pair)
    barrier = pltpu.get_barrier_semaphore()
    peers = [core_peer, mid_peer] + [top_peer(d) for d in range(1, tops)]
    for peer in peers:
        pl.semaphore_signal(
            barrier, inc=1, device_id={"ctx": peer}, device_id_type=pl.DeviceIdType.MESH
        )

    def remote(src, dst, send_sem, recv_sem, peer):
        return pltpu.make_async_remote_copy(
            src_ref=src,
            dst_ref=dst,
            send_sem=send_sem,
            recv_sem=recv_sem,
            device_id={"ctx": peer},
            device_id_type=pl.DeviceIdType.MESH,
        )

    def merge_copies(kind, i, peer):
        send, recv, stat_send, stat_recv, ss, rs = kind
        return (
            remote(send.at[i], recv.at[i], ss.at[0, i], rs.at[0, i], peer),
            remote(stat_send.at[i], stat_recv.at[i], ss.at[1, i], rs.at[1, i], peer),
        )

    core_kind = (core_send, core_recv, core_stat_send, core_stat_recv, core_ss, core_rs)
    mid_kind = (mid_send, mid_recv, mid_stat_send, mid_stat_recv, mid_ss, mid_rs)
    top_kind = (top_send, top_recv, top_stat_send, top_stat_recv, top_ss, top_rs)
    sent = []

    gain = math.log2(math.e) / math.sqrt(HD)
    stat_row = lax.broadcasted_iota(jnp.int32, (8, 128), 0)

    def pack(peak, total):
        return jnp.where(stat_row < 4, peak, total)

    def join(parts):
        top_peak = functools.reduce(jnp.maximum, [p for _, p, _ in parts])
        num, total = None, None
        for n, p, t in parts:
            factor = jnp.exp2((p - top_peak) * gain)
            n, t = n * factor, t * factor
            num, total = (n, t) if num is None else (num + n, total + t)
        return num, top_peak, total

    def received(kind, i, peer):
        for copy in merge_copies(kind, i, peer):
            copy.wait_recv()
        return kind[1][i].astype(jnp.float32), kind[3][i, 0:1, :], kind[3][i, 4:5, :]

    def give(kind, i, peer, part):
        kind[0][i] = part[0].astype(kind[0].dtype)
        kind[2][i] = pack(part[1], part[2])
        for copy in merge_copies(kind, i, peer):
            copy.start()
            sent.append(copy)

    def ready(i):
        for copy in loads[i]:
            copy.wait()
        for copy in w_loads[i] if i + 2 >= chips else list(loads[i + 2]) + w_loads[i]:
            copy.start()
        if i == 0:
            for copy in ints:
                copy.wait()

    def scores_of(i):
        q = jnp.concatenate(
            [q_s[i, side, :, g * HD : (g + 1) * HD] for side in range(2) for g in range(half_heads)],
            axis=0,
        )
        return lax.dot_general(
            k_s[i], q, (((1,), (1,)), ((), ())), preferred_element_type=jnp.float32
        )

    def attend(i, scores):
        if i + 1 < chips:
            ready(i + 1)
        own_count = lens_ref[me]
        later = scores_of(i + 1) if i + 1 < chips else None
        pos = lax.broadcasted_iota(jnp.int32, scores.shape, 0)
        scores = jnp.where(pos < own_count, scores, -jnp.inf)
        peak = jnp.max(scores, axis=0, keepdims=True)
        expo = jnp.exp2((scores - peak) * gain)
        total = jnp.sum(expo, axis=0, keepdims=True)
        num = lax.dot_general(
            v_s[i],
            expo.astype(jnp.bfloat16),
            (((0,), (0,)), ((), ())),
            preferred_element_type=jnp.float32,
        )
        cut = half_heads * num_rows
        num_own[i] = num[:, :cut]
        stat_own[i] = pack(peak[:, :cut], total[:, :cut])
        if i == 0:
            pl.semaphore_wait(barrier, len(peers))
        give(core_kind, i, core_peer, (num[:, cut:], peak[:, cut:], total[:, cut:]))
        return later

    def own_part(i):
        return num_own[i], stat_own[i, 0:1, :], stat_own[i, 4:5, :]

    def settle(i):
        flip, d = order[i]
        part = join([own_part(i), received(core_kind, i, core_peer)])
        slot = d
        if flip:
            give(mid_kind, slot, mid_peer, part)
            return None
        part = join([part, received(mid_kind, slot, mid_peer)])
        if d:
            give(top_kind, d - 1, top_peer(d), part)
            return None
        return part

    ready(0)
    scores = scores_of(0)
    for i in range(chips):
        scores = attend(i, scores)
        if i:
            settle(i - 1)
    part = settle(chips - 1)
    part = join([part] + [received(top_kind, d - 1, top_peer(d)) for d in range(1, tops)])
    merged_t = part[0] / part[2]
    merged = jnp.transpose(merged_t)
    merged = jnp.concatenate(
        [merged[h * num_rows : (h + 1) * num_rows] for h in range(half_heads)], axis=1
    ).astype(jnp.bfloat16)

    def picks(shape, row_axis):
        row = lax.broadcasted_iota(jnp.int32, shape, row_axis)
        place = lax.broadcasted_iota(jnp.int32, shape, 1 - row_axis)
        before, seat = jnp.int32(0), jnp.full(shape, -1, jnp.int32)
        for b in range(NBATCH):
            count = counts_ref[b]
            inside = row - b * BATCH_ROWS
            here = jnp.logical_and(inside >= 0, jnp.logical_and(inside < BATCH_ROWS, inside < count))
            seat = jnp.where(here, before + inside, seat)
            before = before + count
        return jnp.where(seat == place, 1.0, 0.0).astype(jnp.bfloat16)

    merged = jnp.dot(
        picks((LIVE_ROWS, num_rows), 1), merged, preferred_element_type=jnp.float32
    ).astype(jnp.bfloat16)

    def term(i, side):
        w_loads[i][side].wait()
        return jnp.dot(merged, w_s[i, side], preferred_element_type=jnp.float32)

    def term_copy(kind, i, peer):
        send, recv, ss, rs = kind
        return remote(send.at[i], recv.at[i], ss.at[i], rs.at[i], peer)

    tcore_kind = (tcore_send, tcore_recv, tcore_ss, tcore_rs)
    tmid_kind = (tmid_send, tmid_recv, tmid_ss, tmid_rs)
    ttop_kind = (ttop_send, ttop_recv, ttop_ss, ttop_rs)

    def give_term(kind, i, peer, value):
        kind[0][i] = value.astype(jnp.bfloat16)
        copy = term_copy(kind, i, peer)
        copy.start()
        sent.append(copy)

    def received_term(kind, i, peer):
        term_copy(kind, i, peer).wait_recv()
        return kind[1][i].astype(jnp.float32)

    def settle_term(i):
        flip, d = order[i]
        value = term_own[i] + received_term(tcore_kind, i, core_peer)
        slot = d
        if flip:
            give_term(tmid_kind, slot, mid_peer, value)
            return None
        value = value + received_term(tmid_kind, slot, mid_peer)
        if d:
            give_term(ttop_kind, d - 1, top_peer(d), value)
            return None
        return value

    for i in range(chips):
        give_term(tcore_kind, i, core_peer, term(i, 0))
        term_own[i] = term(i, 1)
        if i >= 2:
            settle_term(i - 2)
    settle_term(chips - 2)
    value = settle_term(chips - 1)
    for d in range(1, tops):
        value = value + received_term(ttop_kind, d - 1, top_peer(d))
    out_ref[...] = jnp.dot(
        picks((num_rows, LIVE_ROWS), 0),
        value.astype(jnp.bfloat16),
        preferred_element_type=jnp.float32,
    ).astype(out_ref.dtype)
    for copy in sent:
        copy.wait_send()


def fused_on_device(shards, queries, keys, values, valid_len, row_counts, out_weight):
    num_rows = queries.shape[0]
    ctx_rows = keys.shape[0]
    chips = shards // 2
    tops = shards // 4
    half = HEADS // KVH // 2 * HD
    cut = HEADS // KVH // 2 * num_rows
    depth, width = out_weight.shape[0], out_weight.shape[1] // shards
    vmem = pltpu.VMEM
    bf16, f32 = jnp.bfloat16, jnp.float32

    def merge_slots(count, kind=bf16):
        return [
            vmem((count, HD, cut), kind),
            vmem((count, HD, cut), kind),
            vmem((count, 8, cut), f32),
            vmem((count, 8, cut), f32),
        ]

    def term_slots(count):
        return [vmem((count, LIVE_ROWS, width), bf16)] * 2

    dma = pltpu.SemaphoreType.DMA
    return pl.pallas_call(
        functools.partial(fused_kernel, shards),
        out_shape=pltpu.VMEM((num_rows, width), bf16),
        in_specs=[pl.BlockSpec(memory_space=pl.ANY)] * 6,
        out_specs=pl.BlockSpec(memory_space=pltpu.VMEM),
        scratch_shapes=[
            pltpu.SMEM(valid_len.shape, jnp.int32),
            pltpu.SMEM(row_counts.shape, jnp.int32),
            vmem((chips, 2, num_rows, half), bf16),
            vmem((chips, ctx_rows, HD), bf16),
            vmem((chips, ctx_rows, HD), bf16),
            vmem((chips, 2, depth, width), bf16),
            vmem((chips, HD, cut), f32),
            vmem((chips, 8, cut), f32),
        ]
        + merge_slots(chips, f32)
        + merge_slots(tops)
        + merge_slots(tops - 1)
        + [vmem((chips, LIVE_ROWS, width), f32)]
        + term_slots(chips)
        + term_slots(tops)
        + term_slots(tops - 1)
        + [dma((2,)), dma((chips, 2)), dma((chips,)), dma((chips,)), dma((chips, 2))]
        + [dma((2, chips))] * 2
        + [dma((2, tops))] * 2
        + [dma((2, tops - 1))] * 2
        + [dma((chips,))] * 2
        + [dma((tops,))] * 2
        + [dma((tops - 1,))] * 2,
        compiler_params=pltpu.CompilerParams(
            collective_id=0, has_side_effects=True, vmem_limit_bytes=60 << 20
        ),
    )(valid_len, row_counts, queries, keys, values, out_weight)


def solution(mesh):
    shards = mesh.shape["ctx"]
    body = functools.partial(fused_on_device, shards) if shards == 2 * KVH else on_device
    return jax.shard_map(
        body,
        mesh=mesh,
        in_specs=(
            P("groups", None),
            P(("groups", "ctx"), None),
            P(("groups", "ctx"), None),
            P("groups"),
            P("groups"),
            P("ctx", None),
        ),
        out_specs=P("groups", "ctx"),
        check_vma=False,
    )
```
